32 devices in a mesh: sfc: 16 (over z, y, x), lev: 2 (over core).
Axes of the slice: x: 2, y: 2, z: 4, core: 2. Of those that a mesh axis runs over, the one named last changes fastest.
Arguments:
- air_state: float32 [24, 8, 32768], P(None, 'lev', 'sfc'), may hold values from -6 to 6
- metric: float32 [2, 2048], P(None, 'sfc'), may hold values from -5 to 5
- jacobian: float32 [2048], P('sfc'), may hold values from 0.25 to 4
- edge_nbr: int32 [4, 2048], P(None, 'sfc'), may hold values from 0 to 2047, as said below
- edge_side: int32 [4, 2048], P(None, 'sfc'), may hold values from 0 to 3
- coszen: float32 [32768], P('sfc'), may hold values from -1 to 1
- kappa_base: float32 [112], replicated, may hold values from 0.02 to 2
- band_kappa: float32 [112, 20], replicated, may hold values from 0.005 to 0.2
- solar_weight: float32 [112], replicated, may hold values from 0.5 to 2
- stretch_pos: int32 [32768], P('sfc'), may hold values from 0 to 32767, as said below
- stretch_src: int32 [32768], P('sfc'), may hold values from 0 to 32767, as said below
Outputs:
- new_state: float32 [24, 8, 32768], P(None, 'lev', 'sfc')
- surface_flux: float32 [32768], P(('sfc', 'lev'))
The draws below stay inside these ranges and needn't reach their ends.
Inputs may be any that keep to these rules, and one draw needn't show every extreme that they name: edge_nbr[k, g] lies within 128 elements of g along the curve, cyclically over 2048 elements; that distance is reached. stretch_pos is a permutation of the columns and stretch_src its inverse; column c belongs to the stretch of device stretch_pos[c] // 2048; each device receives 2048 columns, at most 256 of them from one device, a bound reached in every draw; the columns that one device sends to one device take consecutive stretch positions. `stretch_src`: the inverse of stretch_pos.
All inputs are finite; a program needn't handle non-finite values.
Results may differ from the reference program's by a relative error of at most 0.0001.
Values sent between devices are 32-bit elements; how exact they have to be, the bound alone decides.
A program may use at most 64 MiB of HBM per device.

```python
import math
import jax
import jax.numpy as jnp
import numpy as np
from jax import lax

NODES = 16
E_DEV = 128
TRACERS = 20
GPOINTS = 112
GBLOCK = 16
FIELDS = 24
LEVELS = 8
ELEMS = 2048
COLS_DEV = 2048
COLUMNS = 32768
N_SFC = 16


def stretch_tables(key):
    sfc_devices = N_SFC
    local_cols = NODES * E_DEV
    even_share = local_cols // sfc_devices
    pair_count = sfc_devices // 2
    key_list = jax.random.split(jax.random.fold_in(key, 7), 3)
    shuffle_order = jax.random.permutation(key_list[0], sfc_devices).astype(jnp.int32)
    amounts = jax.random.randint(key_list[1], (pair_count,), 0, even_share + 1).astype(jnp.int32)
    amounts = amounts.at[0].set(even_share)
    shift_extra = jnp.zeros((sfc_devices,), jnp.int32).at[shuffle_order[0::2]].set(amounts)
    shift_extra = shift_extra.at[shuffle_order[1::2]].set(-amounts)
    source_ids = jnp.arange(sfc_devices, dtype=jnp.int32)[:, None]
    target_ids = jnp.arange(sfc_devices, dtype=jnp.int32)[None, :]
    sizes_table = even_share + shift_extra[jnp.mod(target_ids - source_ids, sfc_devices)]
    inclusive = jnp.cumsum(sizes_table, axis=1).astype(jnp.int32)
    starts = inclusive - sizes_table
    offsets = (jnp.cumsum(sizes_table, axis=0) - sizes_table).astype(jnp.int32)
    slot_range = jnp.arange(local_cols, dtype=jnp.int32)
    destination = jax.vmap(lambda cum_row: jnp.searchsorted(cum_row, slot_range, side='right'))(inclusive).astype(jnp.int32)
    start_of = jnp.take_along_axis(starts, destination, axis=1)
    offset_of = jnp.take_along_axis(offsets, destination, axis=1)
    position = destination * local_cols + offset_of + slot_range[None, :] - start_of
    shuffles = jax.vmap(lambda sub_key: jax.random.permutation(sub_key, local_cols))(jax.random.split(key_list[2], sfc_devices)).astype(jnp.int32)
    column = source_ids * local_cols + shuffles
    all_columns = sfc_devices * local_cols
    forward = jnp.zeros((all_columns,), jnp.int32).at[column.reshape(-1)].set(position.reshape(-1).astype(jnp.int32))
    backward = jnp.zeros((all_columns,), jnp.int32).at[position.reshape(-1)].set(column.reshape(-1))
    return (forward, backward)


def draw_stretch_pos(key, part):
    return stretch_tables(key)[0]


def draw_stretch_src(key, part):
    return stretch_tables(key)[1]


def draw_edge_nbr(key, part):
    element_total = N_SFC * E_DEV
    curve_steps = jax.random.randint(jax.random.fold_in(key, 3), (4, element_total), -E_DEV, E_DEV + 1).astype(jnp.int32)
    curve_steps = curve_steps.at[0, 0].set(E_DEV)
    return jnp.mod(jnp.arange(element_total, dtype=jnp.int32)[None, :] + curve_steps, element_total).astype(jnp.int32)


def set_ends(values, own_key, least, largest):
    longest = values.shape.index(max(values.shape))
    spots = []
    for shift in (0, 1):
        where = [jax.random.randint(jax.random.fold_in(own_key, axis), (), 0, length) for axis, length in enumerate(values.shape)]
        where[longest] = (where[longest] + shift) % values.shape[longest]
        spots.append(tuple(where))
    return values.at[spots[0]].set(least).at[spots[1]].set(largest)


def levels(rng, shape, cuts, low, largest):
    loudness = 1.0
    for axis_at, blocks in cuts:
        draws = jax.random.uniform(jax.random.fold_in(jax.random.fold_in(rng, 6), axis_at), (blocks,), jnp.float32, low / len(cuts), largest / len(cuts))
        loudness = loudness * jnp.repeat(jnp.exp(draws), shape[axis_at] // blocks).reshape((-1,) + (1,) * (len(shape) - 1 - axis_at))
    return loudness


def bell_draw(rng, dims, width, bound, cuts=(), kind=jnp.bfloat16):
    result = jax.random.normal(rng, dims, jnp.float32) * width
    if len(cuts) > 0:
        result = levels(rng, dims, cuts, -0.22, 0.18) * result
    return jnp.clip(result, min=-bound, max=bound).astype(kind)


def setup_inputs(seed: int = 0) -> dict:
    streams_of = jax.random.split(jax.random.key(seed), 12)
    air_state = bell_draw(streams_of[0], (FIELDS, LEVELS, COLUMNS), 1.0, 6.0, ((1, 2), (2, 16)), jnp.float32)
    metric = bell_draw(streams_of[1], (2, ELEMS), 1.0, 5.0, ((1, 16),), jnp.float32)
    jacobian = jnp.clip(jnp.exp(math.log(4.0) - 2.7725887 * jax.random.uniform(streams_of[2], (ELEMS,), jnp.float32) ** levels(streams_of[2], (ELEMS,), ((0, 16),), -0.2, 0.2)), 0.25, 4.0)
    edge_nbr = draw_edge_nbr(jax.random.fold_in(streams_of[11], 71), 0)
    edge_side = set_ends(jax.random.randint(streams_of[4], (4, ELEMS), 0, 4), jax.random.fold_in(streams_of[4], 1), 0, 3).astype(jnp.int32)
    coszen = jnp.clip(jax.random.uniform(streams_of[5], (COLUMNS,), jnp.float32, -1.0, 1.0) * levels(streams_of[5], (COLUMNS,), ((0, 16),), -0.4, 0.0), -1.0, 1.0)
    kappa_base = jnp.clip(jnp.exp(jax.random.uniform(streams_of[6], (GPOINTS,), jnp.float32, math.log(0.02), math.log(2.0))), 0.02, 2.0)
    band_kappa = jnp.clip(jnp.exp(jax.random.uniform(streams_of[7], (GPOINTS, TRACERS), jnp.float32, math.log(0.005), math.log(0.2))), 0.005, 0.2)
    solar_weight = jnp.clip(jnp.exp(jax.random.uniform(streams_of[8], (GPOINTS,), jnp.float32, math.log(0.5), math.log(2.0))), 0.5, 2.0)
    stretch_pos = draw_stretch_pos(jax.random.fold_in(streams_of[11], 71), 0)
    stretch_src = draw_stretch_src(jax.random.fold_in(streams_of[11], 71), 0)
    return dict(air_state=air_state, metric=metric, jacobian=jacobian, edge_nbr=edge_nbr, edge_side=edge_side, coszen=coszen, kappa_base=kappa_base, band_kappa=band_kappa, solar_weight=solar_weight, stretch_pos=stretch_pos, stretch_src=stretch_src)


GLL_POINTS = np.array([-1.0, -1.0 / np.sqrt(5.0), 1.0 / np.sqrt(5.0), 1.0])
EDGE_NODES = np.array([[4, 8], [13, 14], [11, 7], [2, 1]], dtype=np.int32)
STEP_DYN = 0.2
DEPTH_UNIT = 0.05
HEAT_SCALE = 0.1
FLUX_SCALE = 0.02

def derivative_tables():
    spacing = GLL_POINTS[:, None] - GLL_POINTS[None, :]
    unit_diag = np.eye(4)
    safe_space = np.where(unit_diag > 0, 1.0, spacing)
    weights_row = np.prod(safe_space, axis=1)
    derivative = weights_row[:, None] / weights_row[None, :] / safe_space
    inverse_gap = np.where(unit_diag > 0, 0.0, 1.0 / safe_space)
    derivative = np.where(unit_diag > 0, inverse_gap.sum(axis=1)[:, None], derivative)
    along_i = np.kron(derivative, np.eye(4))
    along_j = np.kron(np.eye(4), derivative)
    return (jnp.asarray(along_i, jnp.float32), jnp.asarray(along_j, jnp.float32))

def advance(element_grid, metric, rows_i, rows_j, start):
    first_term = jnp.einsum('an,flne->flae', rows_i, element_grid, precision=lax.Precision.HIGHEST)
    second_term = jnp.einsum('an,flne->flae', rows_j, element_grid, precision=lax.Precision.HIGHEST)
    return start + STEP_DYN * (metric[0] * first_term + metric[1] * second_term)

def radiate(tracers, sun_angle, kappa_base, band_kappa, solar_weight):
    squares = tracers * tracers
    groups = kappa_base.shape[0] // GBLOCK
    level_count = tracers.shape[1]
    column_count = tracers.shape[2]

    def one_group(running, pieces):
        base_rate, rate_rows, bright = pieces
        absorb = jnp.einsum('gt,tln->gln', rate_rows, squares, precision=lax.Precision.HIGHEST) + base_rate[:, None, None]
        layer_depth = absorb * DEPTH_UNIT
        depth_above = jnp.cumsum(layer_depth, axis=1) - layer_depth
        heating = jnp.einsum('g,gln->ln', bright, jnp.exp(-depth_above) * (1.0 - jnp.exp(-layer_depth)), precision=lax.Precision.HIGHEST)
        ground = jnp.einsum('g,gn->n', bright, jnp.exp(-(depth_above[:, -1] + layer_depth[:, -1])), precision=lax.Precision.HIGHEST)
        return ((running[0] + heating, running[1] + ground), None)
    start_vals = (jnp.zeros((level_count, column_count), jnp.float32), jnp.zeros((column_count,), jnp.float32))
    stacked = (kappa_base.reshape(groups, GBLOCK), band_kappa.reshape(groups, GBLOCK, -1), solar_weight.reshape(groups, GBLOCK))
    (heating, ground), _ = lax.scan(one_group, start_vals, stacked)
    sun_height = jnp.maximum(sun_angle, 0.0)
    return (HEAT_SCALE * sun_height * heating, FLUX_SCALE * sun_height * ground)

def reference(air_state, metric, jacobian, edge_nbr, edge_side, coszen, kappa_base, band_kappa, solar_weight, stretch_pos, stretch_src):
    field_count, level_count, all_cols = air_state.shape
    along_i, along_j = derivative_tables()
    element_grid = air_state.reshape(field_count, level_count, N_SFC, NODES, E_DEV).transpose(0, 1, 3, 2, 4).reshape(field_count, level_count, NODES, ELEMS)
    advanced = advance(element_grid, metric, along_i, along_j, element_grid)
    edge_flat = jnp.asarray(EDGE_NODES.reshape(-1))
    own_values = advanced[:, :, edge_flat]
    node_pick = jnp.asarray(EDGE_NODES[:, ::-1].copy())[edge_side]
    far_values = advanced[:, :, node_pick, edge_nbr[:, :, None]]
    far_values = far_values.transpose(0, 1, 2, 4, 3).reshape(field_count, level_count, 8, ELEMS)
    far_jac = jnp.broadcast_to(jacobian[edge_nbr][:, None, :], (4, 2, ELEMS)).reshape(8, ELEMS)
    summed = (jacobian * own_values + far_jac * far_values) / (jacobian + far_jac)
    dynamic = advanced.at[:, :, edge_flat].set(summed)
    dynamic = dynamic.reshape(field_count, level_count, NODES, N_SFC, E_DEV).transpose(0, 1, 3, 2, 4).reshape(field_count, level_count, all_cols)
    stretch_tracers = jnp.take(dynamic[4:], stretch_src, axis=2)
    stretch_sun = coszen[stretch_src]
    tracer_blocks = stretch_tracers.reshape(TRACERS, level_count, N_SFC, COLS_DEV).transpose(2, 0, 1, 3)
    sun_blocks = stretch_sun.reshape(N_SFC, COLS_DEV)

    def per_block(block_pair):
        return radiate(block_pair[0], block_pair[1], kappa_base, band_kappa, solar_weight)
    heating, ground = lax.map(per_block, (tracer_blocks, sun_blocks))
    heating = heating.transpose(1, 0, 2).reshape(level_count, all_cols)
    surface_flux = ground.reshape(-1)
    heat_cols = jnp.take(heating, stretch_pos, axis=1)
    new_state = dynamic.at[2].add(heat_cols)
    return (new_state, surface_flux)
```

```python
import functools

import jax
import jax.numpy as jnp
import numpy as np
from jax import lax
from jax.experimental import pallas as pl
from jax.experimental.pallas import tpu as pltpu
from jax.sharding import PartitionSpec as P

NODES = 16
GLL_POINTS = np.array([-1.0, -1.0 / np.sqrt(5.0), 1.0 / np.sqrt(5.0), 1.0])
EDGE_NODES = ((4, 8), (13, 14), (11, 7), (2, 1))
STEP_DYN = 0.2
DEPTH_UNIT = 0.05
HEAT_SCALE = 0.1
FLUX_SCALE = 0.02
F32 = jnp.float32
BF16 = jnp.bfloat16


def derivative_matrix():
    spacing = GLL_POINTS[:, None] - GLL_POINTS[None, :]
    unit_diag = np.eye(4)
    safe_space = np.where(unit_diag > 0, 1.0, spacing)
    weights_row = np.prod(safe_space, axis=1)
    derivative = weights_row[:, None] / weights_row[None, :] / safe_space
    inverse_gap = np.where(unit_diag > 0, 0.0, 1.0 / safe_space)
    return np.where(unit_diag > 0, inverse_gap.sum(axis=1)[:, None], derivative)


def split2(x):
    high = x.astype(BF16)
    return high, (x - high.astype(F32)).astype(BF16)


def dot(a, b):
    return jnp.dot(a, b, preferred_element_type=F32)


def advance_kernel(x_ref, metric_ref, adv_ref, edge_ref):
    rows, cols = x_ref.shape
    ne = cols // NODES
    d = derivative_matrix()
    m0 = jnp.broadcast_to(STEP_DYN * metric_ref[0:1, :], (8, ne))
    m1 = jnp.broadcast_to(STEP_DYN * metric_ref[1:2, :], (8, ne))

    def step(r, carry):
        sl = pl.ds(pl.multiple_of(r * 8, 8), 8)
        x = [x_ref[sl, n * ne : (n + 1) * ne] for n in range(NODES)]
        out = []
        for i in range(4):
            for j in range(4):
                first = sum(float(d[i, a]) * x[4 * a + j] for a in range(4))
                second = sum(float(d[j, a]) * x[4 * i + a] for a in range(4))
                out.append(x[4 * i + j] + (m0 * first + m1 * second))
        for n in range(NODES):
            adv_ref[sl, n * ne : (n + 1) * ne] = out[n]
        low = pl.ds(pl.multiple_of(rows + r * 8, 8), 8)
        for k, (a, b) in enumerate(EDGE_NODES):
            edge_ref[sl, k * ne : (k + 1) * ne] = out[b]
            edge_ref[low, k * ne : (k + 1) * ne] = out[a]
        return carry

    lax.fori_loop(0, rows // 8, step, 0)


def edge_kernel(
    levels, adv_ref, own_ref, left_ref, right_ref, jac_ref, target_ref, dyn_ref, sq_ref
):
    rows, cols = adv_ref.shape
    ne = cols // NODES
    fields = rows // levels
    width = 4 * ne
    target = target_ref[...]
    acc = jnp.zeros((2 * rows + 16, width), F32)
    for w, ref in enumerate((left_ref, own_ref, right_ref)):
        lanes = lax.broadcasted_iota(jnp.int32, (width, width), 0) + w * width
        onehot = jnp.where(lanes == target, 1.0, 0.0).astype(BF16)
        jac = jnp.concatenate([jac_ref[w : w + 1, :]] * 4, axis=1)
        src = jnp.concatenate([ref[...], jnp.broadcast_to(jac, (16, width))], axis=0)
        high, low = split2(src)
        acc = acc + dot(high, onehot) + dot(low, onehot)
    own_jac = jnp.concatenate([jac_ref[1:2, :]] * 4, axis=1)
    far_jac = acc[2 * rows : 2 * rows + 1, :]
    total = own_jac + far_jac
    own_part, far_part = own_jac / total, far_jac / total
    first = own_part * own_ref[rows:, :] + far_part * acc[:rows]
    second = own_part * own_ref[:rows, :] + far_part * acc[rows : 2 * rows]
    where = {}
    for k, (a, b) in enumerate(EDGE_NODES):
        where[a], where[b] = (first, k), (second, k)
    for n in range(NODES):
        sl = slice(n * ne, (n + 1) * ne)
        if n in where:
            values, k = where[n]
            piece = values[:, k * ne : (k + 1) * ne]
        else:
            piece = adv_ref[:, sl]
        dyn_ref[:, sl] = piece
        squares = piece * piece
        sq_ref[:, sl] = sum(squares[l * fields : (l + 1) * fields] for l in range(levels))


def physics_kernel(
    levels, top_ref, dyn_ref, own_ref, other_ref, rate_ref, base_ref, weight_ref, sun_ref, out_ref, flux_ref
):
    fields = dyn_ref.shape[0] // levels
    top = top_ref[0]
    rates, base, weight = rate_ref[...], base_ref[...], weight_ref[...]
    other = other_ref[...]

    def light(sums, count):
        high = sums.astype(BF16).astype(F32)
        stacked = jnp.concatenate([high, sums - high, high], axis=0).astype(BF16)
        depth = dot(rates, stacked) + count * base
        return jnp.sum(weight * jnp.exp(depth), axis=0, keepdims=True)

    sun = jnp.maximum(sun_ref[...], 0.0)
    extra = light(other + top * own_ref[...], levels * (1.0 + top))
    above = top * jnp.sum(weight) + (1.0 - top) * extra
    running = (1.0 - top) * other
    out_ref[...] = dyn_ref[...]
    for l in range(levels):
        part = dyn_ref[l * fields : (l + 1) * fields, :]
        running = running + part * part
        below = light(running, (1.0 - top) * levels + (l + 1.0))
        row = l * fields + 2
        out_ref[row : row + 1, :] = dyn_ref[row : row + 1, :] + HEAT_SCALE * sun * (above - below)
        above = below
    flux_ref[...] = FLUX_SCALE * sun * (top * extra + (1.0 - top) * above)


def lookup_kernel(table_ref, index_ref, out_ref):
    rows = table_ref.shape[0]
    count = index_ref.shape[1]
    index = index_ref[...]
    high_index, lane_index = index >> 7, index & 127
    onehot = jnp.where(
        lax.broadcasted_iota(jnp.int32, (rows, count), 0) == high_index, 1.0, 0.0
    ).astype(BF16)
    table = table_ref[...].T
    high, rest = split2(table)
    low, tail = split2(table - high.astype(F32))
    picked = dot(high, onehot) + dot(low, onehot) + dot(tail, onehot)
    mask = lax.broadcasted_iota(jnp.int32, (128, count), 0) == lane_index
    out_ref[...] = jnp.sum(jnp.where(mask, picked, 0.0), axis=0, keepdims=True)


def local(
    air_state,
    metric,
    jacobian,
    edge_nbr,
    edge_side,
    coszen,
    kappa_base,
    band_kappa,
    solar_weight,
    stretch_pos,
    stretch_src,
):
    fields, levels, cols = air_state.shape
    ne = cols // NODES
    rows = fields * levels
    count = lax.axis_size("sfc")
    forward = [(i, (i + 1) % count) for i in range(count)]
    backward = [((i + 1) % count, i) for i in range(count)]
    sds = jax.ShapeDtypeStruct

    state = air_state.transpose(1, 0, 2).reshape(rows, cols)
    jac = jacobian[None, :]
    jac3 = jnp.concatenate(
        [lax.ppermute(jac, "sfc", forward), jac, lax.ppermute(jac, "sfc", backward)], axis=0
    )
    near = jnp.mod(edge_nbr - (lax.axis_index("sfc") - 1) * ne, ne * count)
    target = (near // ne) * (4 * ne) + edge_side * ne + near % ne

    advanced, edges = pl.pallas_call(
        advance_kernel,
        out_shape=(sds((rows, cols), F32), sds((2 * rows, 4 * ne), F32)),
        name="advance",
    )(state, metric)
    left = lax.ppermute(edges, "sfc", forward)
    right = lax.ppermute(edges, "sfc", backward)
    dynamic, squares = pl.pallas_call(
        functools.partial(edge_kernel, levels),
        out_shape=(sds((rows, cols), F32), sds((fields, cols), F32)),
        name="edges",
    )(advanced, edges, left, right, jac3, target.reshape(1, 4 * ne))
    other = lax.ppermute(squares, "lev", [(0, 1), (1, 0)])

    rates = jnp.pad(-DEPTH_UNIT * band_kappa, ((0, 0), (fields - band_kappa.shape[1], 0)))
    high = lax.reduce_precision(rates, 8, 7)
    low = lax.reduce_precision(rates - high, 8, 7)
    stacked_rates = jnp.concatenate([high, high, low], axis=1).astype(BF16)
    points = kappa_base.shape[0]
    top = (lax.axis_index("lev") == 0).astype(F32).reshape(1)
    chunk = min(cols, 512)
    whole = lambda shape: pl.BlockSpec(shape, lambda i: (0, 0))
    block = lambda height: pl.BlockSpec((height, chunk), lambda i: (0, i))
    updated, flux = pl.pallas_call(
        functools.partial(physics_kernel, levels),
        grid=(cols // chunk,),
        in_specs=[
            pl.BlockSpec(memory_space=pltpu.SMEM),
            block(rows),
            block(fields),
            block(fields),
            whole((points, 3 * fields)),
            whole((points, 1)),
            whole((points, 1)),
            block(1),
        ],
        out_specs=(block(rows), block(1)),
        out_shape=(sds((rows, cols), F32), sds((1, cols), F32)),
        name="physics",
    )(
        top,
        dynamic,
        squares,
        other,
        stacked_rates,
        -DEPTH_UNIT * kappa_base[:, None],
        solar_weight[:, None],
        coszen[None, :],
    )
    new_state = updated.reshape(levels, fields, cols).transpose(1, 0, 2)

    table = lax.all_to_all(
        jnp.broadcast_to(flux.reshape(1, cols // 128, 128), (count, cols // 128, 128)),
        "sfc",
        split_axis=0,
        concat_axis=0,
        tiled=True,
    ).reshape(count * cols // 128, 128)
    part = cols // lax.axis_size("lev")
    index = lax.dynamic_slice_in_dim(stretch_src, lax.axis_index("lev") * part, part)
    surface_flux = pl.pallas_call(
        lookup_kernel, out_shape=sds((1, part), F32), name="lookup"
    )(table, index[None, :])
    return (new_state, surface_flux.reshape(part))


def solution(mesh):
    return jax.shard_map(
        local,
        mesh=mesh,
        in_specs=(
            P(None, "lev", "sfc"),
            P(None, "sfc"),
            P("sfc"),
            P(None, "sfc"),
            P(None, "sfc"),
            P("sfc"),
            P(),
            P(),
            P(),
            P("sfc"),
            P("sfc"),
        ),
        out_specs=(P(None, "lev", "sfc"), P(("sfc", "lev"))),
        check_vma=False,
    )
```

```python
import functools

import jax
import jax.numpy as jnp
import numpy as np
from jax import lax
from jax.experimental import pallas as pl
from jax.experimental.pallas import tpu as pltpu
from jax.sharding import PartitionSpec as P

NODES = 16
GLL_POINTS = np.array([-1.0, -1.0 / np.sqrt(5.0), 1.0 / np.sqrt(5.0), 1.0])
EDGE_NODES = ((4, 8), (13, 14), (11, 7), (2, 1))
STEP_DYN = 0.2
DEPTH_UNIT = 0.05
HEAT_SCALE = 0.1
FLUX_SCALE = 0.02
F32 = jnp.float32
BF16 = jnp.bfloat16


def derivative_matrix():
    spacing = GLL_POINTS[:, None] - GLL_POINTS[None, :]
    unit_diag = np.eye(4)
    safe_space = np.where(unit_diag > 0, 1.0, spacing)
    weights_row = np.prod(safe_space, axis=1)
    derivative = weights_row[:, None] / weights_row[None, :] / safe_space
    inverse_gap = np.where(unit_diag > 0, 0.0, 1.0 / safe_space)
    return np.where(unit_diag > 0, inverse_gap.sum(axis=1)[:, None], derivative)


def split2(x):
    high = x.astype(BF16)
    return high, (x - high.astype(F32)).astype(BF16)


def dot(a, b):
    return jnp.dot(a, b, preferred_element_type=F32)


MESH = pl.DeviceIdType.MESH
EDGES = tuple(n for pair in EDGE_NODES for n in pair)
INNER = tuple(n for n in range(NODES) if n not in EDGES)


def column(row):
    n = row.shape[1]
    same = lax.broadcasted_iota(jnp.int32, (n, n), 0) == lax.broadcasted_iota(
        jnp.int32, (n, n), 1
    )
    return jnp.sum(jnp.where(same, jnp.broadcast_to(row, (n, n)), 0.0), axis=1, keepdims=True)


def spread_rates(bands, fields):
    tracers = bands.shape[1]
    high, low = split2(-DEPTH_UNIT * bands)
    shape = (tracers, 3 * fields)
    first = lax.broadcasted_iota(jnp.int32, shape, 0) + (fields - tracers)
    lane = lax.broadcasted_iota(jnp.int32, shape, 1)
    pick_high = (lane == first) | (lane == first + fields)
    pick_low = lane == first + 2 * fields
    one = lambda m: jnp.where(m, 1.0, 0.0).astype(BF16)
    return (dot(high, one(pick_high)) + dot(low, one(pick_low))).astype(BF16)


def step_kernel(
    count,
    levels,
    x_ref,
    metric_ref,
    jac_ref,
    nbr_ref,
    side_ref,
    sun_ref,
    base_ref,
    band_ref,
    weight_ref,
    src_ref,
    out_ref,
    flux_ref,
    adv,
    edges,
    left_buf,
    right_buf,
    sq,
    other_sq,
    flux,
    table,
    edge_send,
    edge_recv,
    swap_send,
    swap_recv,
    flux_send,
    flux_recv,
):
    rows, cols = x_ref.shape
    ne = cols // NODES
    fields = rows // levels
    width = 4 * ne
    me, lev = lax.axis_index("sfc"), lax.axis_index("lev")
    after, before = lax.rem(me + 1, count), lax.rem(me + count - 1, count)

    barrier = pltpu.get_barrier_semaphore()

    def greet(step, carry):
        pl.semaphore_signal(
            barrier, inc=1, device_id=(lax.rem(me + step, count), lev), device_id_type=MESH
        )
        return carry

    lax.fori_loop(1, count, greet, 0)
    pl.semaphore_signal(barrier, inc=1, device_id=(me, 1 - lev), device_id_type=MESH)

    d = derivative_matrix()
    m0 = jnp.broadcast_to(STEP_DYN * metric_ref[0:1, :], (8, ne))
    m1 = jnp.broadcast_to(STEP_DYN * metric_ref[1:2, :], (8, ne))
    for k in range(4):
        edges[2 * rows :, k * ne : (k + 1) * ne] = jnp.broadcast_to(jac_ref[...], (8, ne))

    def advance(r, carry):
        sl = pl.ds(pl.multiple_of(r * 8, 8), 8)
        x = [x_ref[sl, n * ne : (n + 1) * ne] for n in range(NODES)]
        out = []
        for i in range(4):
            for j in range(4):
                first = sum(float(d[i, a]) * x[4 * a + j] for a in range(4))
                second = sum(float(d[j, a]) * x[4 * i + a] for a in range(4))
                out.append(x[4 * i + j] + (m0 * first + m1 * second))
        for n in INNER:
            adv[sl, n * ne : (n + 1) * ne] = out[n]
        low = pl.ds(pl.multiple_of(rows + r * 8, 8), 8)
        for k, (a, b) in enumerate(EDGE_NODES):
            edges[sl, k * ne : (k + 1) * ne] = out[b]
            edges[low, k * ne : (k + 1) * ne] = out[a]
        return carry

    lax.fori_loop(0, rows // 8, advance, 0)
    pl.semaphore_wait(barrier, count)

    to_after = pltpu.make_async_remote_copy(
        edges, left_buf, edge_send.at[0], edge_recv.at[0], device_id=(after, lev), device_id_type=MESH
    )
    to_before = pltpu.make_async_remote_copy(
        edges, right_buf, edge_send.at[1], edge_recv.at[1], device_id=(before, lev), device_id_type=MESH
    )
    to_after.start()
    to_before.start()

    def swap(half):
        return pltpu.make_async_remote_copy(
            sq.at[half],
            other_sq.at[half],
            swap_send.at[half],
            swap_recv.at[half],
            device_id=(me, 1 - lev),
            device_id_type=MESH,
        )

    def put_squares(half, slot, piece):
        squares = piece * piece
        sq[half, :, slot * ne : (slot + 1) * ne] = sum(
            squares[l * fields : (l + 1) * fields] for l in range(levels)
        )

    for slot, n in enumerate(INNER):
        put_squares(0, slot, adv[:, n * ne : (n + 1) * ne])
    inner_swap = swap(0)
    inner_swap.start()

    top = jnp.where(lev == 0, 1.0, 0.0).astype(F32)
    rates = spread_rates(band_ref[...], fields)
    base = -DEPTH_UNIT * column(base_ref[...])
    weight = column(weight_ref[...])
    whole_light = jnp.sum(weight)

    total_nodes = count * ne
    near = nbr_ref[...] - (me - 1) * ne
    near = jnp.where(near < 0, near + total_nodes, near)
    near = jnp.where(near >= total_nodes, near - total_nodes, near)
    window = jnp.where(near >= ne, 1, 0) + jnp.where(near >= 2 * ne, 1, 0)
    spot = window * (width - ne) + side_ref[...] * ne + near
    target = jnp.concatenate([spot[k : k + 1, :] for k in range(4)], axis=1)

    def gather(ref, w):
        lanes = lax.broadcasted_iota(jnp.int32, (width, width), 0) + w * width
        onehot = jnp.where(lanes == target, 1.0, 0.0).astype(BF16)
        high, low = split2(ref[...])
        return dot(high, onehot) + dot(low, onehot)

    def light(sums, times):
        high = sums.astype(BF16).astype(F32)
        stacked = jnp.concatenate([high, sums - high, high], axis=0).astype(BF16)
        depth = dot(rates, stacked) + times * base
        return jnp.sum(weight * jnp.exp(depth), axis=0, keepdims=True)

    def radiate(half, slots, nodes, pieces):
        lanes = slice(slots[0] * ne, (slots[-1] + 1) * ne)
        join = lambda parts: jnp.concatenate(parts, axis=1)
        sun = jnp.maximum(join([sun_ref[:, n * ne : (n + 1) * ne] for n in nodes]), 0.0)
        other = other_sq[half, :, lanes]
        extra = light(other + top * sq[half, :, lanes], levels * (1.0 + top))
        above = top * whole_light + (1.0 - top) * extra
        running = (1.0 - top) * other
        for l in range(levels):
            part = join([p[l * fields : (l + 1) * fields, :] for p in pieces])
            running = running + part * part
            below = light(running, (1.0 - top) * levels + (l + 1.0))
            heat = HEAT_SCALE * sun * (above - below)
            row = l * fields + 2
            for s, n in enumerate(nodes):
                out_ref[row : row + 1, n * ne : (n + 1) * ne] = (
                    pieces[s][row : row + 1, :] + heat[:, s * ne : (s + 1) * ne]
                )
            above = below
        ground = FLUX_SCALE * sun * (top * extra + (1.0 - top) * above)
        for s, n in enumerate(nodes):
            flux[n : n + 1, :] = ground[:, s * ne : (s + 1) * ne]

    acc = gather(edges, 1)
    inner_swap.wait()
    for part in range(2):
        slots = range(part * 4, part * 4 + 4)
        nodes = [INNER[s] for s in slots]
        pieces = [adv[:, n * ne : (n + 1) * ne] for n in nodes]
        for n, piece in zip(nodes, pieces):
            out_ref[:, n * ne : (n + 1) * ne] = piece
        radiate(0, slots, nodes, pieces)

    to_after.wait()
    acc = acc + gather(left_buf, 0)
    to_before.wait()
    acc = acc + gather(right_buf, 2)

    own_jac = jnp.concatenate([jac_ref[...]] * 4, axis=1)
    far_jac = acc[2 * rows : 2 * rows + 1, :]
    total = own_jac + far_jac
    own_part, far_part = own_jac / total, far_jac / total
    first = own_part * edges[rows : 2 * rows, :] + far_part * acc[:rows]
    second = own_part * edges[:rows, :] + far_part * acc[rows : 2 * rows]
    sets = ((first, [a for a, _ in EDGE_NODES]), (second, [b for _, b in EDGE_NODES]))
    for part, (values, nodes) in enumerate(sets):
        for k, n in enumerate(nodes):
            piece = values[:, k * ne : (k + 1) * ne]
            put_squares(1, part * 4 + k, piece)
            out_ref[:, n * ne : (n + 1) * ne] = piece
    edge_swap = swap(1)
    edge_swap.start()
    edge_swap.wait()
    for part, (_, nodes) in enumerate(sets):
        slots = range(part * 4, part * 4 + 4)
        radiate(1, slots, nodes, [out_ref[:, n * ne : (n + 1) * ne] for n in nodes])

    def send(step):
        return pltpu.make_async_remote_copy(
            flux,
            table.at[me],
            flux_send.at[step],
            flux_recv.at[me],
            device_id=(lax.rem(me + step, count), lev),
            device_id_type=MESH,
        )

    def arrive(step):
        peer = lax.rem(me + step, count)
        return pltpu.make_async_remote_copy(
            flux,
            table.at[peer],
            flux_send.at[step],
            flux_recv.at[peer],
            device_id=(peer, lev),
            device_id_type=MESH,
        )

    def start_send(step, carry):
        send(step).start()
        return carry

    def finish(step, carry):
        send(step).wait_send()
        arrive(step).wait_recv()
        return carry

    lax.fori_loop(1, count, start_send, 0)
    table[me] = flux[...]
    taken = flux_ref.shape[1]
    index = src_ref[:, pl.ds(pl.multiple_of(lev * taken, 128), taken)]
    high_index, lane_index = index >> 7, index & 127
    lines = count * cols // 128
    onehot = jnp.where(
        lax.broadcasted_iota(jnp.int32, (lines, taken), 0) == high_index, 1.0, 0.0
    ).astype(BF16)
    mask = lax.broadcasted_iota(jnp.int32, (128, taken), 0) == lane_index
    lax.fori_loop(1, count, finish, 0)
    values = table[...].reshape(lines, 128).T
    high, _ = split2(values)
    low, tail = split2(values - high.astype(F32))
    picked = dot(high, onehot) + dot(low, onehot) + dot(tail, onehot)
    flux_ref[...] = jnp.sum(jnp.where(mask, picked, 0.0), axis=0, keepdims=True)


def local(
    air_state,
    metric,
    jacobian,
    edge_nbr,
    edge_side,
    coszen,
    kappa_base,
    band_kappa,
    solar_weight,
    stretch_pos,
    stretch_src,
):
    fields, levels, cols = air_state.shape
    ne = cols // NODES
    rows = fields * levels
    count = lax.axis_size("sfc")
    part = cols // lax.axis_size("lev")
    state = air_state.transpose(1, 0, 2).reshape(rows, cols)
    vmem = pl.BlockSpec(memory_space=pltpu.VMEM)
    new, flux = pl.pallas_call(
        functools.partial(step_kernel, count, levels),
        in_specs=[vmem] * 10,
        out_specs=(vmem, vmem),
        out_shape=(
            jax.ShapeDtypeStruct((rows, cols), F32),
            jax.ShapeDtypeStruct((1, part), F32),
        ),
        scratch_shapes=[
            pltpu.VMEM((rows, cols), F32),
            pltpu.VMEM((2 * rows + 8, 4 * ne), F32),
            pltpu.VMEM((2 * rows + 8, 4 * ne), F32),
            pltpu.VMEM((2 * rows + 8, 4 * ne), F32),
            pltpu.VMEM((2, fields, cols // 2), F32),
            pltpu.VMEM((2, fields, cols // 2), F32),
            pltpu.VMEM((NODES, ne), F32),
            pltpu.VMEM((count, NODES, ne), F32),
            pltpu.SemaphoreType.DMA((2,)),
            pltpu.SemaphoreType.DMA((2,)),
            pltpu.SemaphoreType.DMA((2,)),
            pltpu.SemaphoreType.DMA((2,)),
            pltpu.SemaphoreType.DMA((count,)),
            pltpu.SemaphoreType.DMA((count,)),
        ],
        compiler_params=pltpu.CompilerParams(collective_id=0, has_side_effects=True),
        name="step",
    )(
        state,
        metric,
        jacobian[None, :],
        edge_nbr,
        edge_side,
        coszen[None, :],
        kappa_base[None, :],
        band_kappa,
        solar_weight[None, :],
        stretch_src[None, :],
    )
    new_state = new.reshape(levels, fields, cols).transpose(1, 0, 2)
    return (new_state, flux.reshape(part))


def solution(mesh):
    return jax.shard_map(
        local,
        mesh=mesh,
        in_specs=(
            P(None, "lev", "sfc"),
            P(None, "sfc"),
            P("sfc"),
            P(None, "sfc"),
            P(None, "sfc"),
            P("sfc"),
            P(),
            P(),
            P(),
            P("sfc"),
            P("sfc"),
        ),
        out_specs=(P(None, "lev", "sfc"), P(("sfc", "lev"))),
        check_vma=False,
    )
```

```python
import functools

import jax
import jax.numpy as jnp
import numpy as np
from jax import lax
from jax.experimental import pallas as pl
from jax.experimental.pallas import tpu as pltpu
from jax.sharding import PartitionSpec as P

NODES = 16
GLL_POINTS = np.array([-1.0, -1.0 / np.sqrt(5.0), 1.0 / np.sqrt(5.0), 1.0])
EDGE_NODES = ((4, 8), (13, 14), (11, 7), (2, 1))
STEP_DYN = 0.2
DEPTH_UNIT = 0.05
HEAT_SCALE = 0.1
FLUX_SCALE = 0.02
F32 = jnp.float32
BF16 = jnp.bfloat16


def derivative_matrix():
    spacing = GLL_POINTS[:, None] - GLL_POINTS[None, :]
    unit_diag = np.eye(4)
    safe_space = np.where(unit_diag > 0, 1.0, spacing)
    weights_row = np.prod(safe_space, axis=1)
    derivative = weights_row[:, None] / weights_row[None, :] / safe_space
    inverse_gap = np.where(unit_diag > 0, 0.0, 1.0 / safe_space)
    return np.where(unit_diag > 0, inverse_gap.sum(axis=1)[:, None], derivative)


def split2(x):
    high = x.astype(BF16)
    return high, (x - high.astype(F32)).astype(BF16)


def dot(a, b):
    return jnp.dot(a, b, preferred_element_type=F32)


MESH = pl.DeviceIdType.MESH
EDGES = tuple(n for pair in EDGE_NODES for n in pair)
INNER = tuple(n for n in range(NODES) if n not in EDGES)


def column(row):
    n = row.shape[1]
    same = lax.broadcasted_iota(jnp.int32, (n, n), 0) == lax.broadcasted_iota(
        jnp.int32, (n, n), 1
    )
    return jnp.sum(jnp.where(same, jnp.broadcast_to(row, (n, n)), 0.0), axis=1, keepdims=True)


def spread_rates(bands, fields):
    tracers = bands.shape[0]
    high, low = split2(-DEPTH_UNIT * bands)
    shape = (tracers, 3 * fields)
    first = lax.broadcasted_iota(jnp.int32, shape, 0) + (fields - tracers)
    lane = lax.broadcasted_iota(jnp.int32, shape, 1)
    pick_high = (lane == first) | (lane == first + fields)
    pick_low = lane == first + 2 * fields
    one = lambda m: jnp.where(m, 1.0, 0.0).astype(BF16)
    mix = lambda a, b: lax.dot_general(a, b, (((0,), (0,)), ((), ())), preferred_element_type=F32)
    return (mix(high, one(pick_high)) + mix(low, one(pick_low))).astype(BF16)


def step_kernel(
    count,
    levels,
    x_ref,
    metric_ref,
    jac_ref,
    nbr_ref,
    side_ref,
    sun_ref,
    base_ref,
    band_ref,
    weight_ref,
    src_ref,
    out_ref,
    flux_ref,
    adv,
    edges,
    direct_buf,
    relay_buf,
    sq,
    other_sq,
    flux,
    table,
    edge_send,
    edge_recv,
    swap_send,
    swap_recv,
    flux_send,
    flux_recv,
):
    rows, cols = x_ref.shape
    ne = cols // NODES
    fields = rows // levels
    width = 4 * ne
    me, lev = lax.axis_index("sfc"), lax.axis_index("lev")
    odd = lax.rem(me, 2)
    partner = me + 1 - 2 * odd
    onward = lax.rem(me + count + 2 - 4 * odd, count)

    barrier = pltpu.get_barrier_semaphore()

    def greet(step, carry):
        pl.semaphore_signal(
            barrier, inc=1, device_id=(lax.rem(me + step, count), lev), device_id_type=MESH
        )
        return carry

    lax.fori_loop(1, count, greet, 0)
    pl.semaphore_signal(barrier, inc=1, device_id=(me, 1 - lev), device_id_type=MESH)

    d = derivative_matrix()
    m0 = jnp.broadcast_to(STEP_DYN * metric_ref[0:1, :], (8, ne))
    m1 = jnp.broadcast_to(STEP_DYN * metric_ref[1:2, :], (8, ne))
    for k in range(4):
        edges[:8, k * ne : (k + 1) * ne] = jnp.broadcast_to(jac_ref[...], (8, ne))

    def chunk(l):
        return slice(0 if l == 0 else 8 + 2 * fields * l, 8 + 2 * fields * (l + 1))

    def direct(l):
        return pltpu.make_async_remote_copy(
            edges.at[chunk(l)],
            direct_buf.at[chunk(l)],
            edge_send.at[0, l],
            edge_recv.at[0, l],
            device_id=(partner, lev),
            device_id_type=MESH,
        )

    def relay(l):
        return pltpu.make_async_remote_copy(
            direct_buf.at[chunk(l)],
            relay_buf.at[chunk(l)],
            edge_send.at[1, l],
            edge_recv.at[1, l],
            device_id=(onward, lev),
            device_id_type=MESH,
        )

    for l in range(levels):

        def advance(r, carry, l=l):
            sl = pl.ds(pl.multiple_of(l * fields + r * 8, 8), 8)
            x = [x_ref[sl, n * ne : (n + 1) * ne] for n in range(NODES)]
            out = []
            for i in range(4):
                for j in range(4):
                    one = sum(float(d[i, a]) * x[4 * a + j] for a in range(4))
                    two = sum(float(d[j, a]) * x[4 * i + a] for a in range(4))
                    out.append(x[4 * i + j] + (m0 * one + m1 * two))
            for n in INNER:
                adv[sl, n * ne : (n + 1) * ne] = out[n]
            start = 8 + 2 * fields * l + r * 8
            seconds = pl.ds(pl.multiple_of(start, 8), 8)
            firsts = pl.ds(pl.multiple_of(start + fields, 8), 8)
            for k, (a, b) in enumerate(EDGE_NODES):
                edges[seconds, k * ne : (k + 1) * ne] = out[b]
                edges[firsts, k * ne : (k + 1) * ne] = out[a]
            return carry

        lax.fori_loop(0, fields // 8, advance, 0)
        if l == 0:
            pl.semaphore_wait(barrier, count)
        direct(l).start()

    def swap(half):
        return pltpu.make_async_remote_copy(
            sq.at[half],
            other_sq.at[half],
            swap_send.at[half],
            swap_recv.at[half],
            device_id=(me, 1 - lev),
            device_id_type=MESH,
        )

    def put_squares(half, slot, piece):
        squares = piece * piece
        sq[half, :, slot * ne : (slot + 1) * ne] = sum(
            squares[l * fields : (l + 1) * fields] for l in range(levels)
        )

    for slot, n in enumerate(INNER):
        put_squares(0, slot, adv[:, n * ne : (n + 1) * ne])
    inner_swap = swap(0)
    inner_swap.start()

    top = jnp.where(lev == 0, 1.0, 0.0).astype(F32)
    rates = spread_rates(band_ref[...], fields)
    base = -DEPTH_UNIT * column(base_ref[...])
    weight = column(weight_ref[...])
    whole_light = jnp.sum(weight)

    total_nodes = count * ne
    near = nbr_ref[...] - (me - 1) * ne
    near = jnp.where(near < 0, near + total_nodes, near)
    near = jnp.where(near >= total_nodes, near - total_nodes, near)
    window = jnp.where(near >= ne, 1, 0) + jnp.where(near >= 2 * ne, 1, 0)
    spot = window * (width - ne) + side_ref[...] * ne + near
    target = jnp.concatenate([spot[k : k + 1, :] for k in range(4)], axis=1)

    def choice(w):
        lanes = lax.broadcasted_iota(jnp.int32, (width, width), 0) + w * width
        return jnp.where(lanes == target, 1.0, 0.0).astype(BF16)

    def gather(ref, onehot, l):
        high, low = split2(ref[chunk(l)])
        return dot(high, onehot) + dot(low, onehot)

    def light(sums, times):
        high = sums.astype(BF16).astype(F32)
        stacked = jnp.concatenate([high, sums - high, high], axis=0).astype(BF16)
        depth = dot(rates, stacked) + times * base
        return jnp.sum(weight * jnp.exp(depth), axis=0, keepdims=True)

    def radiate(half, slots, nodes, pieces):
        lanes = slice(slots[0] * ne, (slots[-1] + 1) * ne)
        join = lambda parts: jnp.concatenate(parts, axis=1)
        sun = jnp.maximum(join([sun_ref[:, n * ne : (n + 1) * ne] for n in nodes]), 0.0)
        other = other_sq[half, :, lanes]
        extra = light(other + top * sq[half, :, lanes], levels * (1.0 + top))
        above = top * whole_light + (1.0 - top) * extra
        running = (1.0 - top) * other
        for l in range(levels):
            part = join([p[l * fields : (l + 1) * fields, :] for p in pieces])
            running = running + part * part
            below = light(running, (1.0 - top) * levels + (l + 1.0))
            heat = HEAT_SCALE * sun * (above - below)
            row = l * fields + 2
            for s, n in enumerate(nodes):
                out_ref[row : row + 1, n * ne : (n + 1) * ne] = (
                    pieces[s][row : row + 1, :] + heat[:, s * ne : (s + 1) * ne]
                )
            above = below
        ground = FLUX_SCALE * sun * (top * extra + (1.0 - top) * above)
        for s, n in enumerate(nodes):
            flux[n : n + 1, :] = ground[:, s * ne : (s + 1) * ne]

    def forward(l):
        direct(l).wait_recv()
        relay(l).start()

    own_choice = choice(1)
    acc = [gather(edges, own_choice, l) for l in range(levels)]
    forward(0)
    inner_swap.wait()
    for part in range(2):
        slots = range(part * 4, part * 4 + 4)
        nodes = [INNER[s] for s in slots]
        pieces = [adv[:, n * ne : (n + 1) * ne] for n in nodes]
        for n, piece in zip(nodes, pieces):
            out_ref[:, n * ne : (n + 1) * ne] = piece
        radiate(0, slots, nodes, pieces)
        if part == 0:
            forward(1)

    direct_choice, relay_choice = choice(2 - 2 * odd), choice(2 * odd)
    for l in range(levels):
        if l > 1:
            forward(l)
        acc[l] = acc[l] + gather(direct_buf, direct_choice, l)

    firsts = [a for a, _ in EDGE_NODES]
    seconds = [b for _, b in EDGE_NODES]
    sums = [0.0, 0.0]
    for l in range(levels):
        relay(l).wait_recv()
        far = acc[l] + gather(relay_buf, relay_choice, l)
        if l == 0:
            own_jac = jnp.concatenate([jac_ref[...]] * 4, axis=1)
            far_jac = far[0:1, :]
            far = far[8:]
            total = own_jac + far_jac
            own_part, far_part = own_jac / total, far_jac / total
        start = 8 + 2 * fields * l
        own_second = edges[start : start + fields, :]
        own_first = edges[start + fields : start + 2 * fields, :]
        both = (
            (own_part * own_first + far_part * far[:fields], firsts),
            (own_part * own_second + far_part * far[fields:], seconds),
        )
        for p, (values, nodes) in enumerate(both):
            sums[p] = sums[p] + values * values
            for k, n in enumerate(nodes):
                out_ref[l * fields : (l + 1) * fields, n * ne : (n + 1) * ne] = values[
                    :, k * ne : (k + 1) * ne
                ]
    sq[1, :, :width] = sums[0]
    sq[1, :, width:] = sums[1]
    edge_swap = swap(1)
    edge_swap.start()
    edge_swap.wait()
    for part, nodes in enumerate((firsts, seconds)):
        slots = range(part * 4, part * 4 + 4)
        radiate(1, slots, nodes, [out_ref[:, n * ne : (n + 1) * ne] for n in nodes])

    def send(step):
        return pltpu.make_async_remote_copy(
            flux,
            table.at[me],
            flux_send.at[step],
            flux_recv.at[me],
            device_id=(lax.rem(me + step, count), lev),
            device_id_type=MESH,
        )

    def arrive(step):
        peer = lax.rem(me + step, count)
        return pltpu.make_async_remote_copy(
            flux,
            table.at[peer],
            flux_send.at[step],
            flux_recv.at[peer],
            device_id=(peer, lev),
            device_id_type=MESH,
        )

    def start_send(step, carry):
        send(step).start()
        return carry

    def finish(step, carry):
        send(step).wait_send()
        arrive(step).wait_recv()
        return carry

    lax.fori_loop(1, count, start_send, 0)
    table[me] = flux[...]
    taken = flux_ref.shape[1]
    index = src_ref[:, pl.ds(pl.multiple_of(lev * taken, 128), taken)]
    high_index, lane_index = index >> 7, index & 127
    lines = count * cols // 128
    onehot = jnp.where(
        lax.broadcasted_iota(jnp.int32, (lines, taken), 0) == high_index, 1.0, 0.0
    ).astype(BF16)
    mask = lax.broadcasted_iota(jnp.int32, (128, taken), 0) == lane_index
    lax.fori_loop(1, count, finish, 0)
    for l in range(levels):
        direct(l).wait_send()
        relay(l).wait_send()
    values = table[...].reshape(lines, 128).T
    high, _ = split2(values)
    low, tail = split2(values - high.astype(F32))
    picked = dot(high, onehot) + dot(low, onehot) + dot(tail, onehot)
    flux_ref[...] = jnp.sum(jnp.where(mask, picked, 0.0), axis=0, keepdims=True)


def local(
    air_state,
    metric,
    jacobian,
    edge_nbr,
    edge_side,
    coszen,
    kappa_base,
    band_kappa,
    solar_weight,
    stretch_pos,
    stretch_src,
):
    fields, levels, cols = air_state.shape
    ne = cols // NODES
    rows = fields * levels
    count = lax.axis_size("sfc")
    part = cols // lax.axis_size("lev")
    state = air_state.transpose(1, 0, 2).reshape(rows, cols)
    vmem = pl.BlockSpec(memory_space=pltpu.VMEM)
    new, flux = pl.pallas_call(
        functools.partial(step_kernel, count, levels),
        in_specs=[vmem] * 10,
        out_specs=(vmem, vmem),
        out_shape=(
            jax.ShapeDtypeStruct((rows, cols), F32),
            jax.ShapeDtypeStruct((1, part), F32),
        ),
        scratch_shapes=[
            pltpu.VMEM((rows, cols), F32),
            pltpu.VMEM((2 * rows + 8, 4 * ne), F32),
            pltpu.VMEM((2 * rows + 8, 4 * ne), F32),
            pltpu.VMEM((2 * rows + 8, 4 * ne), F32),
            pltpu.VMEM((2, fields, cols // 2), F32),
            pltpu.VMEM((2, fields, cols // 2), F32),
            pltpu.VMEM((NODES, ne), F32),
            pltpu.VMEM((count, NODES, ne), F32),
            pltpu.SemaphoreType.DMA((2, levels)),
            pltpu.SemaphoreType.DMA((2, levels)),
            pltpu.SemaphoreType.DMA((2,)),
            pltpu.SemaphoreType.DMA((2,)),
            pltpu.SemaphoreType.DMA((count,)),
            pltpu.SemaphoreType.DMA((count,)),
        ],
        compiler_params=pltpu.CompilerParams(collective_id=0, has_side_effects=True),
        name="step",
    )(
        state,
        metric,
        jacobian[None, :],
        edge_nbr,
        edge_side,
        coszen[None, :],
        kappa_base[None, :],
        band_kappa.T,
        solar_weight[None, :],
        stretch_src[None, :],
    )
    new_state = new.reshape(levels, fields, cols).transpose(1, 0, 2)
    return (new_state, flux.reshape(part))


def solution(mesh):
    return jax.shard_map(
        local,
        mesh=mesh,
        in_specs=(
            P(None, "lev", "sfc"),
            P(None, "sfc"),
            P("sfc"),
            P(None, "sfc"),
            P(None, "sfc"),
            P("sfc"),
            P(),
            P(),
            P(),
            P("sfc"),
            P("sfc"),
        ),
        out_specs=(P(None, "lev", "sfc"), P(("sfc", "lev"))),
        check_vma=False,
    )
```

```python
import functools

import jax
import jax.numpy as jnp
import numpy as np
from jax import lax
from jax.experimental import pallas as pl
from jax.experimental.pallas import tpu as pltpu
from jax.sharding import PartitionSpec as P

NODES = 16
GLL_POINTS = np.array([-1.0, -1.0 / np.sqrt(5.0), 1.0 / np.sqrt(5.0), 1.0])
EDGE_NODES = ((4, 8), (13, 14), (11, 7), (2, 1))
STEP_DYN = 0.2
DEPTH_UNIT = 0.05
HEAT_SCALE = 0.1
FLUX_SCALE = 0.02
F32 = jnp.float32
BF16 = jnp.bfloat16


def derivative_matrix():
    spacing = GLL_POINTS[:, None] - GLL_POINTS[None, :]
    unit_diag = np.eye(4)
    safe_space = np.where(unit_diag > 0, 1.0, spacing)
    weights_row = np.prod(safe_space, axis=1)
    derivative = weights_row[:, None] / weights_row[None, :] / safe_space
    inverse_gap = np.where(unit_diag > 0, 0.0, 1.0 / safe_space)
    return np.where(unit_diag > 0, inverse_gap.sum(axis=1)[:, None], derivative)


def split2(x):
    high = x.astype(BF16)
    return high, (x - high.astype(F32)).astype(BF16)


def dot(a, b):
    return jnp.dot(a, b, preferred_element_type=F32)


MESH = pl.DeviceIdType.MESH
EDGES = tuple(n for pair in EDGE_NODES for n in pair)
INNER = tuple(n for n in range(NODES) if n not in EDGES)


def column(row):
    n = row.shape[1]
    same = lax.broadcasted_iota(jnp.int32, (n, n), 0) == lax.broadcasted_iota(
        jnp.int32, (n, n), 1
    )
    return jnp.sum(jnp.where(same, jnp.broadcast_to(row, (n, n)), 0.0), axis=1, keepdims=True)


def spread_rates(bands, fields):
    tracers = bands.shape[0]
    high, low = split2(-DEPTH_UNIT * bands)
    shape = (tracers, 3 * fields)
    first = lax.broadcasted_iota(jnp.int32, shape, 0) + (fields - tracers)
    lane = lax.broadcasted_iota(jnp.int32, shape, 1)
    pick_high = (lane == first) | (lane == first + fields)
    pick_low = lane == first + 2 * fields
    one = lambda m: jnp.where(m, 1.0, 0.0).astype(BF16)
    mix = lambda a, b: lax.dot_general(a, b, (((0,), (0,)), ((), ())), preferred_element_type=F32)
    return (mix(high, one(pick_high)) + mix(low, one(pick_low))).astype(BF16)


def step_kernel(
    count,
    levels,
    state_ref,
    metric_ref,
    jac_ref,
    nbr_ref,
    side_ref,
    sun_ref,
    base_ref,
    band_ref,
    weight_ref,
    src_ref,
    new_ref,
    flux_ref,
    x_ref,
    out_ref,
    adv,
    edges,
    direct_buf,
    relay_buf,
    sq,
    other_sq,
    flux,
    table,
    edge_send,
    edge_recv,
    swap_send,
    swap_recv,
    flux_send,
    flux_recv,
    in_sem,
    out_sem,
):
    rows, cols = x_ref.shape
    ne = cols // NODES
    fields = rows // levels
    width = 4 * ne
    me, lev = lax.axis_index("sfc"), lax.axis_index("lev")
    odd = lax.rem(me, 2)
    partner = me + 1 - 2 * odd
    onward = lax.rem(me + count + 2 - 4 * odd, count)

    def fetch(l):
        return pltpu.make_async_copy(
            state_ref.at[:, l, :], x_ref.at[l * fields : (l + 1) * fields], in_sem.at[l]
        )

    def store(l):
        return pltpu.make_async_copy(
            out_ref.at[l * fields : (l + 1) * fields], new_ref.at[:, l, :], out_sem.at[l]
        )

    for l in range(levels):
        fetch(l).start()
    barrier = pltpu.get_barrier_semaphore()

    def greet(step, carry):
        pl.semaphore_signal(
            barrier, inc=1, device_id=(lax.rem(me + step, count), lev), device_id_type=MESH
        )
        return carry

    lax.fori_loop(1, count, greet, 0)
    pl.semaphore_signal(barrier, inc=1, device_id=(me, 1 - lev), device_id_type=MESH)

    d = derivative_matrix()
    m0 = jnp.broadcast_to(STEP_DYN * metric_ref[0:1, :], (8, ne))
    m1 = jnp.broadcast_to(STEP_DYN * metric_ref[1:2, :], (8, ne))
    for k in range(4):
        edges[:8, k * ne : (k + 1) * ne] = jnp.broadcast_to(jac_ref[...], (8, ne))

    def chunk(l):
        return slice(0 if l == 0 else 8 + 2 * fields * l, 8 + 2 * fields * (l + 1))

    def direct(l):
        return pltpu.make_async_remote_copy(
            edges.at[chunk(l)],
            direct_buf.at[chunk(l)],
            edge_send.at[0, l],
            edge_recv.at[0, l],
            device_id=(partner, lev),
            device_id_type=MESH,
        )

    def relay(l):
        return pltpu.make_async_remote_copy(
            direct_buf.at[chunk(l)],
            relay_buf.at[chunk(l)],
            edge_send.at[1, l],
            edge_recv.at[1, l],
            device_id=(onward, lev),
            device_id_type=MESH,
        )

    for l in range(levels):

        def advance(r, carry, l=l):
            sl = pl.ds(pl.multiple_of(l * fields + r * 8, 8), 8)
            x = [x_ref[sl, n * ne : (n + 1) * ne] for n in range(NODES)]
            out = []
            for i in range(4):
                for j in range(4):
                    one = sum(float(d[i, a]) * x[4 * a + j] for a in range(4))
                    two = sum(float(d[j, a]) * x[4 * i + a] for a in range(4))
                    out.append(x[4 * i + j] + (m0 * one + m1 * two))
            for n in INNER:
                adv[sl, n * ne : (n + 1) * ne] = out[n]
            start = 8 + 2 * fields * l + r * 8
            seconds = pl.ds(pl.multiple_of(start, 8), 8)
            firsts = pl.ds(pl.multiple_of(start + fields, 8), 8)
            for k, (a, b) in enumerate(EDGE_NODES):
                edges[seconds, k * ne : (k + 1) * ne] = out[b]
                edges[firsts, k * ne : (k + 1) * ne] = out[a]
            return carry

        fetch(l).wait()
        lax.fori_loop(0, fields // 8, advance, 0)
        if l == 0:
            pl.semaphore_wait(barrier, count)
        direct(l).start()

    def swap(half):
        return pltpu.make_async_remote_copy(
            sq.at[half],
            other_sq.at[half],
            swap_send.at[half],
            swap_recv.at[half],
            device_id=(me, 1 - lev),
            device_id_type=MESH,
        )

    def put_squares(half, slot, piece):
        squares = piece * piece
        sq[half, :, slot * ne : (slot + 1) * ne] = sum(
            squares[l * fields : (l + 1) * fields] for l in range(levels)
        )

    for slot, n in enumerate(INNER):
        put_squares(0, slot, adv[:, n * ne : (n + 1) * ne])
    inner_swap = swap(0)
    inner_swap.start()

    top = jnp.where(lev == 0, 1.0, 0.0).astype(F32)
    rates = spread_rates(band_ref[...], fields)
    base = -DEPTH_UNIT * column(base_ref[...])
    weight = column(weight_ref[...])
    whole_light = jnp.sum(weight)

    total_nodes = count * ne
    near = nbr_ref[...] - (me - 1) * ne
    near = jnp.where(near < 0, near + total_nodes, near)
    near = jnp.where(near >= total_nodes, near - total_nodes, near)
    window = jnp.where(near >= ne, 1, 0) + jnp.where(near >= 2 * ne, 1, 0)
    spot = window * (width - ne) + side_ref[...] * ne + near
    target = jnp.concatenate([spot[k : k + 1, :] for k in range(4)], axis=1)

    def choice(w):
        lanes = lax.broadcasted_iota(jnp.int32, (width, width), 0) + w * width
        return jnp.where(lanes == target, 1.0, 0.0).astype(BF16)

    def gather(ref, onehot, l):
        high, low = split2(ref[chunk(l)])
        return dot(high, onehot) + dot(low, onehot)

    def light(sums, times):
        high = sums.astype(BF16).astype(F32)
        stacked = jnp.concatenate([high, sums - high, high], axis=0).astype(BF16)
        depth = dot(rates, stacked) + times * base
        return jnp.sum(weight * jnp.exp(depth), axis=0, keepdims=True)

    def radiate(half, slots, nodes, pieces):
        lanes = slice(slots[0] * ne, (slots[-1] + 1) * ne)
        join = lambda parts: jnp.concatenate(parts, axis=1)
        sun = jnp.maximum(join([sun_ref[:, n * ne : (n + 1) * ne] for n in nodes]), 0.0)
        other = other_sq[half, :, lanes]
        extra = light(other + top * sq[half, :, lanes], levels * (1.0 + top))
        above = top * whole_light + (1.0 - top) * extra
        running = (1.0 - top) * other
        for l in range(levels):
            part = join([p[l * fields : (l + 1) * fields, :] for p in pieces])
            running = running + part * part
            below = light(running, (1.0 - top) * levels + (l + 1.0))
            heat = HEAT_SCALE * sun * (above - below)
            row = l * fields + 2
            for s, n in enumerate(nodes):
                out_ref[row : row + 1, n * ne : (n + 1) * ne] = (
                    pieces[s][row : row + 1, :] + heat[:, s * ne : (s + 1) * ne]
                )
            above = below
        ground = FLUX_SCALE * sun * (top * extra + (1.0 - top) * above)
        for s, n in enumerate(nodes):
            flux[n : n + 1, :] = ground[:, s * ne : (s + 1) * ne]

    def forward(l):
        direct(l).wait_recv()
        relay(l).start()

    own_choice = choice(1)
    acc = [gather(edges, own_choice, l) for l in range(levels)]
    forward(0)
    inner_swap.wait()
    for part in range(2):
        slots = range(part * 4, part * 4 + 4)
        nodes = [INNER[s] for s in slots]
        pieces = [adv[:, n * ne : (n + 1) * ne] for n in nodes]
        for n, piece in zip(nodes, pieces):
            out_ref[:, n * ne : (n + 1) * ne] = piece
        radiate(0, slots, nodes, pieces)
        if part == 0:
            forward(1)

    direct_choice, relay_choice = choice(2 - 2 * odd), choice(2 * odd)
    for l in range(levels):
        if l > 1:
            forward(l)
        acc[l] = acc[l] + gather(direct_buf, direct_choice, l)

    firsts = [a for a, _ in EDGE_NODES]
    seconds = [b for _, b in EDGE_NODES]
    sums = [0.0, 0.0]
    for l in range(levels):
        relay(l).wait_recv()
        far = acc[l] + gather(relay_buf, relay_choice, l)
        if l == 0:
            own_jac = jnp.concatenate([jac_ref[...]] * 4, axis=1)
            far_jac = far[0:1, :]
            far = far[8:]
            total = own_jac + far_jac
            own_part, far_part = own_jac / total, far_jac / total
        start = 8 + 2 * fields * l
        own_second = edges[start : start + fields, :]
        own_first = edges[start + fields : start + 2 * fields, :]
        both = (
            (own_part * own_first + far_part * far[:fields], firsts),
            (own_part * own_second + far_part * far[fields:], seconds),
        )
        for p, (values, nodes) in enumerate(both):
            sums[p] = sums[p] + values * values
            for k, n in enumerate(nodes):
                out_ref[l * fields : (l + 1) * fields, n * ne : (n + 1) * ne] = values[
                    :, k * ne : (k + 1) * ne
                ]
    sq[1, :, :width] = sums[0]
    sq[1, :, width:] = sums[1]
    edge_swap = swap(1)
    edge_swap.start()
    edge_swap.wait()
    for part, nodes in enumerate((firsts, seconds)):
        slots = range(part * 4, part * 4 + 4)
        radiate(1, slots, nodes, [out_ref[:, n * ne : (n + 1) * ne] for n in nodes])

    def send(step):
        return pltpu.make_async_remote_copy(
            flux,
            table.at[me],
            flux_send.at[step],
            flux_recv.at[me],
            device_id=(lax.rem(me + step, count), lev),
            device_id_type=MESH,
        )

    def arrive(step):
        peer = lax.rem(me + step, count)
        return pltpu.make_async_remote_copy(
            flux,
            table.at[peer],
            flux_send.at[step],
            flux_recv.at[peer],
            device_id=(peer, lev),
            device_id_type=MESH,
        )

    def start_send(step, carry):
        send(step).start()
        return carry

    def finish(step, carry):
        send(step).wait_send()
        arrive(step).wait_recv()
        return carry

    lax.fori_loop(1, count, start_send, 0)
    for l in range(levels):
        store(l).start()
    table[me] = flux[...]
    taken = flux_ref.shape[1]
    index = src_ref[:, pl.ds(pl.multiple_of(lev * taken, 128), taken)]
    high_index, lane_index = index >> 7, index & 127
    lines = count * cols // 128
    onehot = jnp.where(
        lax.broadcasted_iota(jnp.int32, (lines, taken), 0) == high_index, 1.0, 0.0
    ).astype(BF16)
    mask = lax.broadcasted_iota(jnp.int32, (128, taken), 0) == lane_index
    lax.fori_loop(1, count, finish, 0)
    for l in range(levels):
        store(l).wait()
        direct(l).wait_send()
        relay(l).wait_send()
    values = table[...].reshape(lines, 128).T
    high, _ = split2(values)
    low, tail = split2(values - high.astype(F32))
    picked = dot(high, onehot) + dot(low, onehot) + dot(tail, onehot)
    flux_ref[...] = jnp.sum(jnp.where(mask, picked, 0.0), axis=0, keepdims=True)


def local(
    air_state,
    metric,
    jacobian,
    edge_nbr,
    edge_side,
    coszen,
    kappa_base,
    band_kappa,
    solar_weight,
    stretch_pos,
    stretch_src,
):
    fields, levels, cols = air_state.shape
    ne = cols // NODES
    rows = fields * levels
    count = lax.axis_size("sfc")
    part = cols // lax.axis_size("lev")
    anywhere = pl.BlockSpec(memory_space=pl.ANY)
    vmem = pl.BlockSpec(memory_space=pltpu.VMEM)
    new, flux = pl.pallas_call(
        functools.partial(step_kernel, count, levels),
        in_specs=[anywhere] + [vmem] * 9,
        out_specs=(anywhere, vmem),
        out_shape=(
            jax.ShapeDtypeStruct(air_state.shape, F32),
            jax.ShapeDtypeStruct((1, part), F32),
        ),
        scratch_shapes=[
            pltpu.VMEM((rows, cols), F32),
            pltpu.VMEM((rows, cols), F32),
            pltpu.VMEM((rows, cols), F32),
            pltpu.VMEM((2 * rows + 8, 4 * ne), F32),
            pltpu.VMEM((2 * rows + 8, 4 * ne), F32),
            pltpu.VMEM((2 * rows + 8, 4 * ne), F32),
            pltpu.VMEM((2, fields, cols // 2), F32),
            pltpu.VMEM((2, fields, cols // 2), F32),
            pltpu.VMEM((NODES, ne), F32),
            pltpu.VMEM((count, NODES, ne), F32),
            pltpu.SemaphoreType.DMA((2, levels)),
            pltpu.SemaphoreType.DMA((2, levels)),
            pltpu.SemaphoreType.DMA((2,)),
            pltpu.SemaphoreType.DMA((2,)),
            pltpu.SemaphoreType.DMA((count,)),
            pltpu.SemaphoreType.DMA((count,)),
            pltpu.SemaphoreType.DMA((levels,)),
            pltpu.SemaphoreType.DMA((levels,)),
        ],
        compiler_params=pltpu.CompilerParams(collective_id=0, has_side_effects=True),
        name="step",
    )(
        air_state,
        metric,
        jacobian[None, :],
        edge_nbr,
        edge_side,
        coszen[None, :],
        kappa_base[None, :],
        band_kappa.T,
        solar_weight[None, :],
        stretch_src[None, :],
    )
    return (new, flux.reshape(part))


def solution(mesh):
    return jax.shard_map(
        local,
        mesh=mesh,
        in_specs=(
            P(None, "lev", "sfc"),
            P(None, "sfc"),
            P("sfc"),
            P(None, "sfc"),
            P(None, "sfc"),
            P("sfc"),
            P(),
            P(),
            P(),
            P("sfc"),
            P("sfc"),
        ),
        out_specs=(P(None, "lev", "sfc"), P(("sfc", "lev"))),
        check_vma=False,
    )
```

```python
import functools

import jax
import jax.numpy as jnp
import numpy as np
from jax import lax
from jax.experimental import pallas as pl
from jax.experimental.pallas import tpu as pltpu
from jax.sharding import PartitionSpec as P

NODES = 16
GLL_POINTS = np.array([-1.0, -1.0 / np.sqrt(5.0), 1.0 / np.sqrt(5.0), 1.0])
EDGE_NODES = ((4, 8), (13, 14), (11, 7), (2, 1))
STEP_DYN = 0.2
DEPTH_UNIT = 0.05
HEAT_SCALE = 0.1
FLUX_SCALE = 0.02
F32 = jnp.float32
BF16 = jnp.bfloat16


def derivative_matrix():
    spacing = GLL_POINTS[:, None] - GLL_POINTS[None, :]
    unit_diag = np.eye(4)
    safe_space = np.where(unit_diag > 0, 1.0, spacing)
    weights_row = np.prod(safe_space, axis=1)
    derivative = weights_row[:, None] / weights_row[None, :] / safe_space
    inverse_gap = np.where(unit_diag > 0, 0.0, 1.0 / safe_space)
    return np.where(unit_diag > 0, inverse_gap.sum(axis=1)[:, None], derivative)


def split2(x):
    high = x.astype(BF16)
    return high, (x - high.astype(F32)).astype(BF16)


def dot(a, b):
    return jnp.dot(a, b, preferred_element_type=F32)


MESH = pl.DeviceIdType.MESH
EDGES = tuple(n for pair in EDGE_NODES for n in pair)
INNER = tuple(n for n in range(NODES) if n not in EDGES)


def column(row):
    n = row.shape[1]
    same = lax.broadcasted_iota(jnp.int32, (n, n), 0) == lax.broadcasted_iota(
        jnp.int32, (n, n), 1
    )
    return jnp.sum(jnp.where(same, jnp.broadcast_to(row, (n, n)), 0.0), axis=1, keepdims=True)


def spread_rates(bands, fields):
    tracers = bands.shape[0]
    high, low = split2(-DEPTH_UNIT * bands)
    shape = (tracers, 3 * fields)
    first = lax.broadcasted_iota(jnp.int32, shape, 0) + (fields - tracers)
    lane = lax.broadcasted_iota(jnp.int32, shape, 1)
    pick_high = (lane == first) | (lane == first + fields)
    pick_low = lane == first + 2 * fields
    one = lambda m: jnp.where(m, 1.0, 0.0).astype(BF16)
    mix = lambda a, b: lax.dot_general(a, b, (((0,), (0,)), ((), ())), preferred_element_type=F32)
    return (mix(high, one(pick_high)) + mix(low, one(pick_low))).astype(BF16)


def step_kernel(
    count,
    levels,
    state_ref,
    metric_ref,
    jac_ref,
    nbr_ref,
    side_ref,
    sun_ref,
    base_ref,
    band_ref,
    weight_ref,
    src_ref,
    new_ref,
    flux_ref,
    x_ref,
    out_ref,
    adv,
    edges,
    direct_buf,
    relay_buf,
    sq,
    other_sq,
    flux,
    table,
    edge_send,
    edge_recv,
    swap_send,
    swap_recv,
    flux_send,
    flux_recv,
    in_sem,
    out_sem,
):
    rows, cols = x_ref.shape
    ne = cols // NODES
    fields = rows // levels
    width = 4 * ne
    me, lev = lax.axis_index("sfc"), lax.axis_index("lev")
    odd = lax.rem(me, 2)
    partner = me + 1 - 2 * odd
    onward = lax.rem(me + count + 2 - 4 * odd, count)

    def fetch(l):
        return pltpu.make_async_copy(
            state_ref.at[:, l, :], x_ref.at[l * fields : (l + 1) * fields], in_sem.at[l]
        )

    def store(l):
        return pltpu.make_async_copy(
            out_ref.at[l * fields : (l + 1) * fields], new_ref.at[:, l, :], out_sem.at[l]
        )

    for l in range(levels):
        fetch(l).start()
    barrier = pltpu.get_barrier_semaphore()

    def greet(step, carry):
        pl.semaphore_signal(
            barrier, inc=1, device_id=(lax.rem(me + step, count), lev), device_id_type=MESH
        )
        return carry

    lax.fori_loop(1, count, greet, 0)
    pl.semaphore_signal(barrier, inc=1, device_id=(me, 1 - lev), device_id_type=MESH)

    d = derivative_matrix()
    m0 = jnp.broadcast_to(STEP_DYN * metric_ref[0:1, :], (8, ne))
    m1 = jnp.broadcast_to(STEP_DYN * metric_ref[1:2, :], (8, ne))
    for k in range(4):
        edges[:8, k * ne : (k + 1) * ne] = jnp.broadcast_to(jac_ref[...], (8, ne))

    def chunk(l):
        return slice(0 if l == 0 else 8 + 2 * fields * l, 8 + 2 * fields * (l + 1))

    def direct(l):
        return pltpu.make_async_remote_copy(
            edges.at[chunk(l)],
            direct_buf.at[chunk(l)],
            edge_send.at[0, l],
            edge_recv.at[0, l],
            device_id=(partner, lev),
            device_id_type=MESH,
        )

    def relay(l):
        return pltpu.make_async_remote_copy(
            direct_buf.at[chunk(l)],
            relay_buf.at[chunk(l)],
            edge_send.at[1, l],
            edge_recv.at[1, l],
            device_id=(onward, lev),
            device_id_type=MESH,
        )

    for l in range(levels):

        def advance(r, carry, l=l):
            sl = pl.ds(pl.multiple_of(l * fields + r * 8, 8), 8)
            x = [x_ref[sl, n * ne : (n + 1) * ne] for n in range(NODES)]
            out = []
            for i in range(4):
                for j in range(4):
                    one = sum(float(d[i, a]) * x[4 * a + j] for a in range(4))
                    two = sum(float(d[j, a]) * x[4 * i + a] for a in range(4))
                    out.append(x[4 * i + j] + (m0 * one + m1 * two))
            for n in INNER:
                adv[sl, n * ne : (n + 1) * ne] = out[n]
            start = 8 + 2 * fields * l + r * 8
            seconds = pl.ds(pl.multiple_of(start, 8), 8)
            firsts = pl.ds(pl.multiple_of(start + fields, 8), 8)
            for k, (a, b) in enumerate(EDGE_NODES):
                edges[seconds, k * ne : (k + 1) * ne] = out[b]
                edges[firsts, k * ne : (k + 1) * ne] = out[a]
            return carry

        fetch(l).wait()
        lax.fori_loop(0, fields // 8, advance, 0)
        if l == 0:
            pl.semaphore_wait(barrier, count)
        direct(l).start()

    def swap(half):
        return pltpu.make_async_remote_copy(
            sq.at[half],
            other_sq.at[half],
            swap_send.at[half],
            swap_recv.at[half],
            device_id=(me, 1 - lev),
            device_id_type=MESH,
        )

    def put_squares(half, slot, piece):
        squares = piece * piece
        sq[half, :, slot * ne : (slot + 1) * ne] = sum(
            squares[l * fields : (l + 1) * fields] for l in range(levels)
        )

    for slot, n in enumerate(INNER):
        put_squares(0, slot, adv[:, n * ne : (n + 1) * ne])
    inner_swap = swap(0)
    inner_swap.start()

    top = jnp.where(lev == 0, 1.0, 0.0).astype(F32)
    rates = spread_rates(band_ref[...], fields)
    base = -DEPTH_UNIT * column(base_ref[...])
    weight = column(weight_ref[...])
    whole_light = jnp.sum(weight)

    total_nodes = count * ne
    near = nbr_ref[...] - (me - 1) * ne
    near = jnp.where(near < 0, near + total_nodes, near)
    near = jnp.where(near >= total_nodes, near - total_nodes, near)
    window = jnp.where(near >= ne, 1, 0) + jnp.where(near >= 2 * ne, 1, 0)
    spot = window * (width - ne) + side_ref[...] * ne + near
    target = jnp.concatenate([spot[k : k + 1, :] for k in range(4)], axis=1)

    def choice(w):
        lanes = lax.broadcasted_iota(jnp.int32, (width, width), 0) + w * width
        return jnp.where(lanes == target, 1.0, 0.0).astype(BF16)

    def gather(ref, onehot, l):
        high, low = split2(ref[chunk(l)])
        return dot(high, onehot) + dot(low, onehot)

    def depth_of(sums):
        high = sums.astype(BF16).astype(F32)
        stacked = jnp.concatenate([high, sums - high, high], axis=0).astype(BF16)
        return dot(rates, stacked)

    def light(depth, times):
        return jnp.sum(weight * jnp.exp(depth + times * base), axis=0, keepdims=True)

    join = lambda parts: jnp.concatenate(parts, axis=1)

    def own_depths(pieces):
        running, depths = 0.0, []
        for l in range(levels):
            part = join([p[l * fields : (l + 1) * fields, :] for p in pieces])
            running = running + part * part
            depths.append(depth_of(running))
        return depths

    def radiate(half, slots, nodes, pieces, depths):
        lanes = slice(slots[0] * ne, (slots[-1] + 1) * ne)
        sun = jnp.maximum(join([sun_ref[:, n * ne : (n + 1) * ne] for n in nodes]), 0.0)
        other = depth_of(other_sq[half, :, lanes])
        extra = light(other + top * depths[-1], levels * (1.0 + top))
        above = top * whole_light + (1.0 - top) * extra
        other = (1.0 - top) * other
        for l in range(levels):
            below = light(other + depths[l], (1.0 - top) * levels + (l + 1.0))
            heat = HEAT_SCALE * sun * (above - below)
            row = l * fields + 2
            for s, n in enumerate(nodes):
                out_ref[row : row + 1, n * ne : (n + 1) * ne] = (
                    pieces[s][row : row + 1, :] + heat[:, s * ne : (s + 1) * ne]
                )
            above = below
        ground = FLUX_SCALE * sun * (top * extra + (1.0 - top) * above)
        for s, n in enumerate(nodes):
            flux[n : n + 1, :] = ground[:, s * ne : (s + 1) * ne]

    def forward(l):
        direct(l).wait_recv()
        relay(l).start()

    own_choice = choice(1)
    acc = [gather(edges, own_choice, l) for l in range(levels)]
    forward(0)
    inner_swap.wait()
    for part in range(2):
        slots = range(part * 4, part * 4 + 4)
        nodes = [INNER[s] for s in slots]
        pieces = [adv[:, n * ne : (n + 1) * ne] for n in nodes]
        for n, piece in zip(nodes, pieces):
            out_ref[:, n * ne : (n + 1) * ne] = piece
        radiate(0, slots, nodes, pieces, own_depths(pieces))
        if part == 0:
            forward(1)

    direct_choice, relay_choice = choice(2 - 2 * odd), choice(2 * odd)
    for l in range(levels):
        if l > 1:
            forward(l)
        acc[l] = acc[l] + gather(direct_buf, direct_choice, l)

    firsts = [a for a, _ in EDGE_NODES]
    seconds = [b for _, b in EDGE_NODES]
    sums = [0.0, 0.0]
    for l in range(levels):
        relay(l).wait_recv()
        far = acc[l] + gather(relay_buf, relay_choice, l)
        if l == 0:
            own_jac = jnp.concatenate([jac_ref[...]] * 4, axis=1)
            far_jac = far[0:1, :]
            far = far[8:]
            total = own_jac + far_jac
            own_part, far_part = own_jac / total, far_jac / total
        start = 8 + 2 * fields * l
        own_second = edges[start : start + fields, :]
        own_first = edges[start + fields : start + 2 * fields, :]
        both = (
            (own_part * own_first + far_part * far[:fields], firsts),
            (own_part * own_second + far_part * far[fields:], seconds),
        )
        for p, (values, nodes) in enumerate(both):
            sums[p] = sums[p] + values * values
            for k, n in enumerate(nodes):
                out_ref[l * fields : (l + 1) * fields, n * ne : (n + 1) * ne] = values[
                    :, k * ne : (k + 1) * ne
                ]
    sq[1, :, :width] = sums[0]
    sq[1, :, width:] = sums[1]
    edge_swap = swap(1)
    edge_swap.start()
    ready = []
    for nodes in (firsts, seconds):
        pieces = [out_ref[:, n * ne : (n + 1) * ne] for n in nodes]
        ready.append((nodes, pieces, own_depths(pieces)))
    edge_swap.wait()
    for part, work in enumerate(ready):
        radiate(1, range(part * 4, part * 4 + 4), *work)

    def send(step):
        return pltpu.make_async_remote_copy(
            flux,
            table.at[me],
            flux_send.at[step],
            flux_recv.at[me],
            device_id=(lax.rem(me + step, count), lev),
            device_id_type=MESH,
        )

    def arrive(step):
        peer = lax.rem(me + step, count)
        return pltpu.make_async_remote_copy(
            flux,
            table.at[peer],
            flux_send.at[step],
            flux_recv.at[peer],
            device_id=(peer, lev),
            device_id_type=MESH,
        )

    def start_send(step, carry):
        send(step).start()
        return carry

    def finish(step, carry):
        send(step).wait_send()
        arrive(step).wait_recv()
        return carry

    lax.fori_loop(1, count, start_send, 0)
    for l in range(levels):
        store(l).start()
    table[me] = flux[...]
    taken = flux_ref.shape[1]
    index = src_ref[:, pl.ds(pl.multiple_of(lev * taken, 128), taken)]
    high_index, lane_index = index >> 7, index & 127
    lines = count * cols // 128
    onehot = jnp.where(
        lax.broadcasted_iota(jnp.int32, (lines, taken), 0) == high_index, 1.0, 0.0
    ).astype(BF16)
    mask = lax.broadcasted_iota(jnp.int32, (128, taken), 0) == lane_index
    lax.fori_loop(1, count, finish, 0)
    for l in range(levels):
        store(l).wait()
        direct(l).wait_send()
        relay(l).wait_send()
    values = table[...].reshape(lines, 128).T
    high, _ = split2(values)
    low, tail = split2(values - high.astype(F32))
    picked = dot(high, onehot) + dot(low, onehot) + dot(tail, onehot)
    flux_ref[...] = jnp.sum(jnp.where(mask, picked, 0.0), axis=0, keepdims=True)


def local(
    air_state,
    metric,
    jacobian,
    edge_nbr,
    edge_side,
    coszen,
    kappa_base,
    band_kappa,
    solar_weight,
    stretch_pos,
    stretch_src,
):
    fields, levels, cols = air_state.shape
    ne = cols // NODES
    rows = fields * levels
    count = lax.axis_size("sfc")
    part = cols // lax.axis_size("lev")
    anywhere = pl.BlockSpec(memory_space=pl.ANY)
    vmem = pl.BlockSpec(memory_space=pltpu.VMEM)
    new, flux = pl.pallas_call(
        functools.partial(step_kernel, count, levels),
        in_specs=[anywhere] + [vmem] * 9,
        out_specs=(anywhere, vmem),
        out_shape=(
            jax.ShapeDtypeStruct(air_state.shape, F32),
            jax.ShapeDtypeStruct((1, part), F32),
        ),
        scratch_shapes=[
            pltpu.VMEM((rows, cols), F32),
            pltpu.VMEM((rows, cols), F32),
            pltpu.VMEM((rows, cols), F32),
            pltpu.VMEM((2 * rows + 8, 4 * ne), F32),
            pltpu.VMEM((2 * rows + 8, 4 * ne), F32),
            pltpu.VMEM((2 * rows + 8, 4 * ne), F32),
            pltpu.VMEM((2, fields, cols // 2), F32),
            pltpu.VMEM((2, fields, cols // 2), F32),
            pltpu.VMEM((NODES, ne), F32),
            pltpu.VMEM((count, NODES, ne), F32),
            pltpu.SemaphoreType.DMA((2, levels)),
            pltpu.SemaphoreType.DMA((2, levels)),
            pltpu.SemaphoreType.DMA((2,)),
            pltpu.SemaphoreType.DMA((2,)),
            pltpu.SemaphoreType.DMA((count,)),
            pltpu.SemaphoreType.DMA((count,)),
            pltpu.SemaphoreType.DMA((levels,)),
            pltpu.SemaphoreType.DMA((levels,)),
        ],
        compiler_params=pltpu.CompilerParams(collective_id=0, has_side_effects=True),
        name="step",
    )(
        air_state,
        metric,
        jacobian[None, :],
        edge_nbr,
        edge_side,
        coszen[None, :],
        kappa_base[None, :],
        band_kappa.T,
        solar_weight[None, :],
        stretch_src[None, :],
    )
    return (new, flux.reshape(part))


def solution(mesh):
    return jax.shard_map(
        local,
        mesh=mesh,
        in_specs=(
            P(None, "lev", "sfc"),
            P(None, "sfc"),
            P("sfc"),
            P(None, "sfc"),
            P(None, "sfc"),
            P("sfc"),
            P(),
            P(),
            P(),
            P("sfc"),
            P("sfc"),
        ),
        out_specs=(P(None, "lev", "sfc"), P(("sfc", "lev"))),
        check_vma=False,
    )
```
